32 devices in a mesh: grp: 2 (over y), ta: 16 (over z, x, core).
Axes of the slice: x: 2, y: 2, z: 4, core: 2. Of those that a mesh axis runs over, the one named last changes fastest.
Arguments:
- perambulator: bfloat16 [2, 16, 768, 2, 512], P('grp', None, 'ta'), parts along dimension 0, may hold values from -1.1953125 to 1.1953125
- batch_columns: int32 [32], P(('grp', 'ta')), parts along dimension 0, may hold values from 1 to 48, 512 in all
- sink_operator: int32 [2, 16], replicated, may hold values from 0 to 1
- sink_elemental: bfloat16 [8, 16, 2, 128, 128], P('grp'), parts along dimension 0, may hold values from -0.375 to 0.375
- source_elemental: bfloat16 [2, 2, 128, 128], P('grp'), parts along dimension 0, may hold values from -0.375 to 0.375
Outputs:
- loops: bfloat16 [32, 2, 512, 512], P(('grp', 'ta')), parts along dimension 0
The draws below stay inside these ranges and needn't reach their ends.
There are 2 independent parts, one for each index of `grp`. The reference program is written for one: setup_inputs(seed, part) draws one part's arguments, and reference() takes and returns one part's arrays. A program takes and returns all parts, laid end to end along the dimension named above; an argument that names none is the same for every part. Nothing has to cross between parts.
Inputs may be any that keep to these rules, and one draw needn't show every extreme that they name: Batch d holds columns starts[d] to starts[d] + batch_columns[d] - 1 of every source and sink time, in order, in its first batch_columns[d] slots; later slots hold nothing that is read. The entries sum to 512 and the largest equals 48.
All inputs are finite; a program needn't handle non-finite values. No bound on the sum of `batch_columns` on one device may be relied on, other than what follows from the above.
Results may differ from the reference program's by a relative error of at most 0.0057.
Values may be sent and summed in bfloat16 or wider, within the bound.
No kernel may reach another device: no remote copies, remote signals or barrier semaphores. Data moves between devices by JAX's collectives and lax.ppermute only.
A program may use at most 64 MiB of HBM per device.

```python
import math
import jax
import jax.numpy as jnp
import numpy as np
from jax import lax

NEV = 128
NSNK = 16
NDISP = 2
ORDER = 512
NSRC = 1
CAPN = 48
SLOTS = 768
NOPS = 4
N_TA = 16


def plant(values, key, low, high):
    longest = values.shape.index(max(values.shape))
    spots = []
    for shift in (0, 1):
        where = [jax.random.randint(jax.random.fold_in(key, axis), (), 0, length) for axis, length in enumerate(values.shape)]
        where[longest] = (where[longest] + shift) % values.shape[longest]
        spots.append(tuple(where))
    return values.at[spots[0]].set(low).at[spots[1]].set(high)


def shard_levels(stream_key, dims, cuts, least, high):
    factor_of, own = 1.0, jax.random.fold_in(stream_key, 6)
    for axis_at, blocks in cuts:
        draws = jnp.exp(jax.random.uniform(jax.random.fold_in(own, axis_at), (blocks,), jnp.float32, least / len(cuts), high / len(cuts)))
        factor_of = factor_of * jnp.repeat(draws, dims[axis_at] // blocks).reshape([-1 if axis == axis_at else 1 for axis in range(len(dims))])
    return factor_of


def profile(amount, total, limit, slope):
    loads = [(1 << 20) // math.isqrt(rank ** slope) + 1 for rank in range(2, amount + 1)]
    surplus, holding = total - limit - (amount - 1), [1] * (amount - 1)
    while surplus > 0:
        candidates = [i for i in range(amount - 1) if holding[i] < limit]
        pool, budget = sum([loads[i] for i in candidates]), surplus
        for i in candidates:
            addition = min(limit - holding[i], max(1, budget * loads[i] // pool), surplus)
            holding[i] = holding[i] + addition
            surplus = surplus - addition
    return np.array([limit] + holding)


def ragged_sizes(stream_key, count, total, limit, slope):
    if count == 2:
        one = jax.random.randint(stream_key, (), max(1, total - limit), min(limit, total - 1) + 1)
        return jnp.stack([one, total - one])
    sizes = jnp.asarray(profile(count, total, limit, slope), jnp.int32)
    twos = (count - 1) // 2
    source_of, sink = sizes[1:1 + 2 * twos:2], sizes[2:2 + 2 * twos:2]
    margin = jnp.minimum(source_of - 1, limit - sink)
    moved = jax.random.randint(jax.random.fold_in(stream_key, 1), (twos,), 0, 1 << 20) % (margin + 1)
    sizes = sizes.at[1:1 + 2 * twos:2].set(source_of - moved).at[2:2 + 2 * twos:2].set(sink + moved)
    return sizes[jax.random.permutation(jax.random.fold_in(stream_key, 2), count)]


def gaussian(rng, extent, deviation, reach, pieces=(), kind=jnp.bfloat16):
    level = shard_levels(rng, extent, pieces, -0.22, 0.18) if pieces else 1.0
    result = jax.random.normal(rng, extent, jnp.float32) * deviation * level
    return jnp.minimum(jnp.maximum(result, -reach), reach).astype(kind)


def setup_inputs(seed: int = 0, part: int = 0) -> dict:
    key_list = jax.random.split(jax.random.key(seed), 6)
    own_keys = jax.random.split(jax.random.fold_in(key_list[5], part), 6)
    perambulator = gaussian(own_keys[0], (NSRC, NSNK, SLOTS, 2, ORDER), 0.2, 1.1953125, ((2, 16),))
    batch_columns = ragged_sizes(own_keys[1], N_TA, ORDER, CAPN, 2).astype(jnp.int32)
    sink_operator = plant(jax.random.randint(key_list[2], (2, NSNK), 0, 2), jax.random.fold_in(key_list[2], 1), 0, 1).astype(jnp.int32)
    sink_elemental = gaussian(own_keys[3], (NOPS, NSNK, 2, NEV, NEV), (2 * NEV) ** -0.5, 0.375)
    source_elemental = gaussian(own_keys[4], (NSRC, 2, NEV, NEV), (2 * NEV) ** -0.5, 0.375)
    return dict(perambulator=perambulator, batch_columns=batch_columns, sink_operator=sink_operator, sink_elemental=sink_elemental, source_elemental=source_elemental)


def spin_signs():
    spin = jnp.arange(4 * NEV, dtype=jnp.int32) // NEV
    return jnp.where(spin < 2, 1.0, -1.0).astype(jnp.float32)


def column_slots(batch_columns):
    starts = jnp.cumsum(batch_columns) - batch_columns
    column = jnp.arange(ORDER, dtype=jnp.int32)
    holder = jnp.sum((starts[None, :] <= column[:, None]).astype(jnp.int32), axis=1) - 1
    first = jnp.take(starts, holder)
    return (holder * CAPN + column - first).astype(jnp.int32)


def product_t(left, right):
    return jnp.dot(left, right.T, preferred_element_type=jnp.float32)


def pair_loop(columns, e_real, e_imag, f_real, f_imag, signs):
    p_real = columns[:, 0, :]
    p_imag = columns[:, 1, :]
    flat_real = p_real.reshape(ORDER * 4, NEV)
    flat_imag = p_imag.reshape(ORDER * 4, NEV)
    x_real = (product_t(flat_real, e_real) - product_t(flat_imag, e_imag)).reshape(ORDER, ORDER)
    x_imag = (product_t(flat_real, e_imag) + product_t(flat_imag, e_real)).reshape(ORDER, ORDER)
    x_real = (x_real * signs[None, :]).astype(jnp.bfloat16)
    x_imag = (x_imag * signs[None, :]).astype(jnp.bfloat16)
    cube_real = p_real.reshape(4, NEV, ORDER).astype(jnp.float32)
    cube_imag = p_imag.reshape(4, NEV, ORDER).astype(jnp.float32)
    fr = f_real.astype(jnp.float32)
    fi = f_imag.astype(jnp.float32)
    y_real = jnp.einsum("ij,sjk->sik", fr, cube_real) + jnp.einsum("ij,sjk->sik", fi, cube_imag)
    y_imag = jnp.einsum("ij,sjk->sik", fi, cube_real) - jnp.einsum("ij,sjk->sik", fr, cube_imag)
    y_real = (y_real * signs[None, None, :]).reshape(ORDER, ORDER).astype(jnp.bfloat16)
    y_imag = (y_imag * signs[None, None, :]).reshape(ORDER, ORDER).astype(jnp.bfloat16)
    left_real = x_real.T
    left_imag = x_imag.T
    m_real = jnp.dot(left_real, y_real, preferred_element_type=jnp.float32) - jnp.dot(left_imag, y_imag, preferred_element_type=jnp.float32)
    m_imag = jnp.dot(left_real, y_imag, preferred_element_type=jnp.float32) + jnp.dot(left_imag, y_real, preferred_element_type=jnp.float32)
    return jnp.stack([m_real, m_imag], 0).astype(jnp.bfloat16)


def reference(perambulator, batch_columns, sink_operator, sink_elemental, source_elemental):
    slot_index = column_slots(batch_columns)
    signs = spin_signs()

    def one_pair(pair_index):
        source = pair_index // NSNK
        sink_time = pair_index % NSNK
        block_pair = perambulator[source, sink_time]
        columns = jnp.take(block_pair, slot_index, axis=0)
        operator = sink_operator[0, sink_time] * NDISP + sink_operator[1, sink_time]
        element = sink_elemental[operator, sink_time]
        source_table = source_elemental[source]
        return pair_loop(columns, element[0], element[1], source_table[0], source_table[1], signs)

    return lax.map(one_pair, jnp.arange(NSRC * NSNK, dtype=jnp.int32))
```

```python
import functools

import jax
import jax.numpy as jnp
from jax import lax
from jax.experimental import pallas as pl
from jax.experimental.pallas import tpu as pltpu
from jax.sharding import PartitionSpec as P

NDISP = 2
SPINS = 4
LARGEST_EXCHANGE = 32

f32 = jnp.float32
bf16 = jnp.bfloat16


def matmul(left, right):
    return jnp.dot(left, right, preferred_element_type=f32)


def operators_kernel(pair_ref, operator_ref, sink_ref, source_ref, f_ref, e_ref, sink, source, sems):
    source_index, sink_index = pair_ref[0], pair_ref[1]
    chosen = operator_ref[0, sink_index] * NDISP + operator_ref[1, sink_index]
    from_sink = pltpu.make_async_copy(sink_ref.at[chosen, sink_index], sink, sems.at[0])
    from_source = pltpu.make_async_copy(source_ref.at[source_index], source, sems.at[1])
    from_sink.start()
    from_source.start()
    n = sink.shape[-1]
    row = lax.broadcasted_iota(jnp.int32, (2 * n, 2 * n), 0)
    col = lax.broadcasted_iota(jnp.int32, (2 * n, 2 * n), 1)
    spread = jnp.where(col == (row % 2) * n + row // 2, 1.0, 0.0).astype(bf16)
    gathered = jnp.where(row == (col % 2) * n + col // 2, 1.0, 0.0).astype(bf16)
    from_source.wait()
    f_real, f_imag = source[0], source[1]
    stacked = (
        jnp.concatenate([jnp.concatenate([f_real, f_imag], 1), jnp.concatenate([-f_imag, f_real], 1)], 0),
        jnp.concatenate([jnp.concatenate([f_imag, -f_real], 1), jnp.concatenate([f_real, f_imag], 1)], 0),
    )
    for part in range(2):
        rows = matmul(spread, stacked[part]).astype(bf16)
        f_ref[2 * n * part : 2 * n * (part + 1), :] = matmul(rows, gathered).astype(bf16)
    from_sink.wait()
    e_real, e_imag = sink[0], sink[1]
    e_ref[:n, :n] = e_real
    e_ref[:n, n:] = -e_imag
    e_ref[n:, :n] = e_imag
    e_ref[n:, n:] = e_real


def operators(pair, sink_operator, sink_elemental, source_elemental):
    n = source_elemental.shape[-1]
    smem = pl.BlockSpec(memory_space=pltpu.SMEM)
    hbm = pl.BlockSpec(memory_space=pl.ANY)
    vmem = pl.BlockSpec(memory_space=pltpu.VMEM)
    return pl.pallas_call(
        operators_kernel,
        out_shape=(jax.ShapeDtypeStruct((4 * n, 2 * n), bf16), jax.ShapeDtypeStruct((2 * n, 2 * n), bf16)),
        in_specs=[smem, smem, hbm, hbm],
        out_specs=(vmem, vmem),
        scratch_shapes=[
            pltpu.VMEM((2, n, n), bf16),
            pltpu.VMEM((2, n, n), bf16),
            pltpu.SemaphoreType.DMA((2,)),
        ],
        cost_estimate=pl.CostEstimate(flops=10**8, bytes_accessed=10**6, transcendentals=0),
        compiler_params=pltpu.CompilerParams(vmem_limit_bytes=8 * 2**20),
        name="operators",
    )(pair, sink_operator, sink_elemental, source_elemental)


def pair_kernel(group_sizes, me_ref, count_ref, *refs):
    blocks = refs[: len(group_sizes)]
    f_ref, e_ref, out_ref, packed, turned, right, middle, starts, sem = refs[len(group_sizes) :]
    spins, order, _, n = packed.shape
    batches = sum(group_sizes)
    me = me_ref[0]

    def running(batch, start):
        starts[batch] = start
        return start + count_ref[batch ^ me]

    lax.fori_loop(0, batches, running, jnp.int32(0))

    def place(block, position):
        count, start = count_ref[position], starts[position ^ me]
        for spin in range(spins):
            pltpu.make_async_copy(
                block.at[pl.ds(0, count), :, pl.ds(n * spin, n)], packed.at[spin, pl.ds(start, count)], sem
            ).start()

    base = 0
    for size, block in zip(group_sizes, blocks):
        if size == 1:
            place(block.at[0], base)
        else:
            lax.fori_loop(0, size, lambda i, c, block=block, base=base: (place(block.at[i], base + i), c)[1], 0)
        base += size
    pltpu.make_async_copy(packed, packed, sem).wait()
    rows = packed.reshape(spins, 2 * order, n)
    for spin in range(spins):
        near = slice(2 * n * spin, 2 * n * (spin + 1))
        column = jnp.concatenate([rows[other, near, :] for other in range(spins)], axis=1)
        product = matmul(f_ref[...], column).astype(bf16)
        right[near, :order] = product[: 2 * n]
        right[near, order:] = product[2 * n :]
    for spin in range(spins):
        turned[n * spin : n * (spin + 1), :] = rows[spin].T
    total = matmul(turned[...], right[...]).astype(bf16)
    half = order // 2
    for spin in range(spins):
        here = slice(n * spin, n * (spin + 1))
        middle[:n] = total[here, :order]
        middle[n:] = total[here, order:]
        result = matmul(e_ref[...], middle[...])
        first, second = result[:, :half], result[:, half:]
        if spin < spins // 2:
            second = -second
        else:
            first = -first
        for part in range(2):
            out_ref[part, here, :half] = first[n * part : n * (part + 1)].astype(bf16)
            out_ref[part, here, half:] = second[n * part : n * (part + 1)].astype(bf16)


def pair_loop(me, counts, blocks, f_matrix, e_matrix, order):
    n = order // SPINS
    smem = pl.BlockSpec(memory_space=pltpu.SMEM)
    hbm = pl.BlockSpec(memory_space=pl.ANY)
    vmem = pl.BlockSpec(memory_space=pltpu.VMEM)
    sizes = tuple(block.shape[0] for block in blocks)
    return pl.pallas_call(
        functools.partial(pair_kernel, sizes),
        out_shape=jax.ShapeDtypeStruct((2, order, order), bf16),
        in_specs=[smem, smem] + [hbm] * len(blocks) + [vmem, vmem],
        out_specs=vmem,
        scratch_shapes=[
            pltpu.VMEM((SPINS, order, 2, n), bf16),
            pltpu.VMEM((order, 2 * order), bf16),
            pltpu.VMEM((2 * order, 2 * order), bf16),
            pltpu.VMEM((2 * n, order), bf16),
            pltpu.SMEM((sum(sizes),), jnp.int32),
            pltpu.SemaphoreType.DMA,
        ],
        cost_estimate=pl.CostEstimate(flops=2 * 10**9, bytes_accessed=3 * 10**6, transcendentals=0),
        compiler_params=pltpu.CompilerParams(vmem_limit_bytes=24 * 2**20),
        name="pair_loop",
    )(me, counts, *blocks, f_matrix, e_matrix)


def local(perambulator, batch_columns, sink_operator, sink_elemental, source_elemental):
    source_count, sink_count, capacity, _, order = perambulator.shape
    devices = lax.axis_size("ta")
    assert source_count * sink_count == devices
    rank = lax.axis_index("ta")
    outgoing = perambulator.reshape(devices, capacity, 2, order)
    if devices <= LARGEST_EXCHANGE and devices & (devices - 1) == 0:
        blocks = [lax.dynamic_slice_in_dim(outgoing, rank, 1)] + [None] * (devices - 1)
        for mask in range(devices - 1, 0, -1):
            block = lax.dynamic_slice_in_dim(outgoing, rank ^ mask, 1)
            blocks[mask] = lax.ppermute(block, "ta", [(i, i ^ mask) for i in range(devices)])
        counts, mask = batch_columns, 1
        while mask < devices:
            other = lax.ppermute(counts, "ta", [(i, i ^ mask) for i in range(devices)])
            counts = jnp.concatenate([counts, other])
            mask *= 2
        me = rank.astype(jnp.int32)
    else:
        blocks = [lax.all_to_all(outgoing, "ta", split_axis=0, concat_axis=0, tiled=True)]
        counts = lax.all_gather(batch_columns, "ta", axis=0, tiled=True)
        me = jnp.int32(0)
    pair = jnp.stack([rank // sink_count, rank % sink_count]).astype(jnp.int32)
    f_matrix, e_matrix = operators(pair, sink_operator, sink_elemental, source_elemental)
    return pair_loop(me.reshape(1), counts, blocks, f_matrix, e_matrix, order)[None]


def solution(mesh):
    placed = (
        P("grp", None, "ta", None, None),
        P(("grp", "ta")),
        P(),
        P("grp", None, None, None, None),
        P("grp", None, None, None),
    )
    return jax.shard_map(
        local,
        mesh=mesh,
        in_specs=placed,
        out_specs=P(("grp", "ta"), None, None, None),
        check_vma=False,
    )
```

```python
import functools

import jax
import jax.numpy as jnp
from jax import lax
from jax.experimental import pallas as pl
from jax.experimental.pallas import tpu as pltpu
from jax.sharding import PartitionSpec as P

NDISP = 2
SPINS = 4
LARGEST_EXCHANGE = 32
LATE = 2

f32 = jnp.float32
bf16 = jnp.bfloat16

SMEM = pl.BlockSpec(memory_space=pltpu.SMEM)
VMEM = pl.BlockSpec(memory_space=pltpu.VMEM)
HBM = pl.BlockSpec(memory_space=pltpu.HBM)


def matmul(left, right):
    return jnp.dot(left, right, preferred_element_type=f32)


def operators_kernel(rank_ref, operator_ref, sink_ref, source_ref, f_ref, e_ref, sink, source, sems):
    sinks = sink_ref.shape[1]
    source_index, sink_index = rank_ref[0] // sinks, rank_ref[0] % sinks
    chosen = operator_ref[0, sink_index] * NDISP + operator_ref[1, sink_index]
    from_sink = pltpu.make_async_copy(sink_ref.at[chosen, sink_index], sink, sems.at[0])
    from_source = pltpu.make_async_copy(source_ref.at[source_index], source, sems.at[1])
    from_sink.start()
    from_source.start()
    n = sink.shape[-1]
    row = lax.broadcasted_iota(jnp.int32, (2 * n, 2 * n), 0)
    col = lax.broadcasted_iota(jnp.int32, (2 * n, 2 * n), 1)
    spread = jnp.where(col == (row % 2) * n + row // 2, 1.0, 0.0).astype(bf16)
    gathered = jnp.where(row == (col % 2) * n + col // 2, 1.0, 0.0).astype(bf16)
    from_source.wait()
    f_real, f_imag = source[0], source[1]
    stacked = (
        jnp.concatenate([jnp.concatenate([f_real, f_imag], 1), jnp.concatenate([-f_imag, f_real], 1)], 0),
        jnp.concatenate([jnp.concatenate([f_imag, -f_real], 1), jnp.concatenate([f_real, f_imag], 1)], 0),
    )
    for part in range(2):
        rows = matmul(spread, stacked[part]).astype(bf16)
        f_ref[2 * n * part : 2 * n * (part + 1), :] = matmul(rows, gathered).astype(bf16)
    from_sink.wait()
    e_real, e_imag = sink[0], sink[1]
    e_ref[:n, :n] = e_real
    e_ref[:n, n:] = -e_imag
    e_ref[n:, :n] = e_imag
    e_ref[n:, n:] = e_real


def operators(rank, sink_operator, sink_elemental, source_elemental):
    n = source_elemental.shape[-1]
    return pl.pallas_call(
        operators_kernel,
        out_shape=(jax.ShapeDtypeStruct((4 * n, 2 * n), bf16), jax.ShapeDtypeStruct((2 * n, 2 * n), bf16)),
        in_specs=[SMEM, SMEM, HBM, HBM],
        out_specs=(VMEM, VMEM),
        scratch_shapes=[
            pltpu.VMEM((2, n, n), bf16),
            pltpu.VMEM((2, n, n), bf16),
            pltpu.SemaphoreType.DMA((2,)),
        ],
        cost_estimate=pl.CostEstimate(flops=10**8, bytes_accessed=10**6, transcendentals=0),
        compiler_params=pltpu.CompilerParams(vmem_limit_bytes=8 * 2**20),
        name="operators",
    )(rank, sink_operator, sink_elemental, source_elemental)


def place_blocks(me, count_ref, groups, blocks, packed, starts):
    spins, _, _, n = packed.shape
    batches = count_ref.shape[0]
    unroll = 8

    def running(batch, start):
        starts[batch] = start
        return start + count_ref[batch ^ me]

    lax.fori_loop(0, batches, running, jnp.int32(0))

    def place(block, position):
        count, start = count_ref[position], starts[position ^ me]

        def one(column, carry):
            value = block[column]
            for spin in range(spins):
                packed[spin, start + column] = value[:, n * spin : n * (spin + 1)]
            return carry

        def several(group, carry):
            for column in range(unroll):
                one(group * unroll + column, carry)
            return carry

        whole = count // unroll
        lax.fori_loop(0, whole, several, 0)
        lax.fori_loop(whole * unroll, count, one, 0)

    for (base, size), block in zip(groups, blocks):
        if size == 1:
            place(block.at[0], base)
        else:

            def each(index, carry, block=block, base=base):
                place(block.at[index], base + index)
                return carry

            lax.fori_loop(0, size, each, 0)


def early_kernel(groups, me_ref, count_ref, *refs):
    blocks = refs[: len(groups)]
    packed, starts = refs[len(groups) :]
    place_blocks(me_ref[0], count_ref, groups, blocks, packed, starts)


def pack_early(me, counts, groups, blocks, order):
    n = order // SPINS
    return pl.pallas_call(
        functools.partial(early_kernel, groups),
        out_shape=jax.ShapeDtypeStruct((SPINS, order, 2, n), bf16),
        in_specs=[SMEM, SMEM] + [VMEM] * len(blocks),
        out_specs=VMEM,
        scratch_shapes=[pltpu.SMEM(counts.shape, jnp.int32)],
        cost_estimate=pl.CostEstimate(flops=10**8, bytes_accessed=10**6, transcendentals=0),
        compiler_params=pltpu.CompilerParams(vmem_limit_bytes=8 * 2**20),
        name="pack_early",
    )(me, counts, *blocks)


def pair_kernel(groups, me_ref, count_ref, *refs):
    blocks = refs[: len(groups)]
    _, f_ref, e_ref, packed, out_ref, turned, right, middle, starts = refs[len(groups) :]
    spins, order, _, n = packed.shape
    place_blocks(me_ref[0], count_ref, groups, blocks, packed, starts)
    rows = packed.reshape(spins, 2 * order, n)
    for spin in range(spins):
        near = slice(2 * n * spin, 2 * n * (spin + 1))
        column = jnp.concatenate([rows[other, near, :] for other in range(spins)], axis=1)
        product = matmul(f_ref[...], column).astype(bf16)
        right[near, :order] = product[: 2 * n]
        right[near, order:] = product[2 * n :]
    for spin in range(spins):
        turned[n * spin : n * (spin + 1), :] = rows[spin].T
    total = matmul(turned[...], right[...]).astype(bf16)
    half = order // 2
    for spin in range(spins):
        here = slice(n * spin, n * (spin + 1))
        middle[spin, :n] = total[here, :order]
        middle[spin, n:] = total[here, order:]
        result = matmul(e_ref[...], middle[spin])
        first, second = result[:, :half], result[:, half:]
        if spin < spins // 2:
            second = -second
        else:
            first = -first
        for part in range(2):
            out_ref[part, here, :half] = first[n * part : n * (part + 1)].astype(bf16)
            out_ref[part, here, half:] = second[n * part : n * (part + 1)].astype(bf16)


def pair_loop(me, counts, groups, blocks, packed, f_matrix, e_matrix):
    spins, order, _, n = packed.shape
    return pl.pallas_call(
        functools.partial(pair_kernel, groups),
        out_shape=(jax.ShapeDtypeStruct(packed.shape, bf16), jax.ShapeDtypeStruct((2, order, order), bf16)),
        in_specs=[SMEM, SMEM] + [VMEM] * (len(blocks) + 3),
        out_specs=(VMEM, VMEM),
        scratch_shapes=[
            pltpu.VMEM((order, 2 * order), bf16),
            pltpu.VMEM((2 * order, 2 * order), bf16),
            pltpu.VMEM((spins, 2 * n, order), bf16),
            pltpu.SMEM(counts.shape, jnp.int32),
        ],
        input_output_aliases={2 + len(blocks): 0},
        cost_estimate=pl.CostEstimate(flops=2 * 10**9, bytes_accessed=3 * 10**6, transcendentals=0),
        compiler_params=pltpu.CompilerParams(vmem_limit_bytes=24 * 2**20),
        name="pair_loop",
    )(me, counts, *blocks, packed, f_matrix, e_matrix)[1]


def exchange_order(devices):
    far = list(range(devices - 1, devices // 2 - 1, -1))
    near = list(range(devices // 2 - 1, 0, -1))
    order = far[:2]
    for index, mask in enumerate(far[2:]):
        order += near[index : index + 1] + [mask]
    return order + near[len(far) - 2 :]


def exchange(outgoing, counts, rank, devices):
    pairs = lambda mask: [(i, i ^ mask) for i in range(devices)]
    top = devices // 2
    masks = exchange_order(devices)
    blocks = [None] * devices
    held, bit = counts, top
    for turn, mask in enumerate(masks):
        block = lax.dynamic_slice_in_dim(outgoing, rank ^ mask, 1)
        if turn == 0:
            outgoing, block = lax.optimization_barrier((outgoing, block))
        if bit:
            moved = lax.ppermute(held, "ta", pairs(bit))
            held = jnp.concatenate([held, moved])
            bit //= 2
        blocks[mask] = lax.ppermute(block, "ta", pairs(mask))
    blocks[0] = lax.dynamic_slice_in_dim(outgoing, rank, 1)
    bits = devices.bit_length() - 1
    counts = held.reshape((2,) * bits).transpose(tuple(range(bits))[::-1]).reshape(devices)
    return blocks, masks, counts


def local(perambulator, batch_columns, sink_operator, sink_elemental, source_elemental):
    source_count, sink_count, capacity, _, order = perambulator.shape
    devices = lax.axis_size("ta")
    assert source_count * sink_count == devices
    rank = lax.axis_index("ta").astype(jnp.int32)
    outgoing = perambulator.reshape(devices, capacity, 2, order)
    if devices <= LARGEST_EXCHANGE and devices & (devices - 1) == 0:
        blocks, masks, counts = exchange(outgoing, batch_columns, rank, devices)
        last = [mask for mask in masks if mask >= devices // 2][-LATE:]
        early = [mask for mask in range(devices) if mask not in last]
        me = rank
    else:
        blocks = [lax.all_to_all(outgoing, "ta", split_axis=0, concat_axis=0, tiled=True)]
        counts = lax.all_gather(batch_columns, "ta", axis=0, tiled=True)
        early, last = [0], []
        me = jnp.int32(0)
    sizes = {block: blocks[block].shape[0] for block in early + last}
    groups = lambda chosen: tuple((block, sizes[block]) for block in chosen)
    me = me.reshape(1)
    f_matrix, e_matrix = operators(rank.reshape(1), sink_operator, sink_elemental, source_elemental)
    packed = pack_early(me, counts, groups(early), [blocks[i] for i in early], order)
    return pair_loop(me, counts, groups(last), [blocks[i] for i in last], packed, f_matrix, e_matrix)[None]


def solution(mesh):
    placed = (
        P("grp", None, "ta", None, None),
        P(("grp", "ta")),
        P(),
        P("grp", None, None, None, None),
        P("grp", None, None, None),
    )
    return jax.shard_map(
        local,
        mesh=mesh,
        in_specs=placed,
        out_specs=P(("grp", "ta"), None, None, None),
        check_vma=False,
    )
```

```python
import functools

import jax
import jax.numpy as jnp
from jax import lax
from jax.experimental import pallas as pl
from jax.experimental.pallas import tpu as pltpu
from jax.sharding import PartitionSpec as P

NDISP = 2
SPINS = 4
LARGEST_EXCHANGE = 32
LEAD = 2

f32 = jnp.float32
bf16 = jnp.bfloat16

SMEM = pl.BlockSpec(memory_space=pltpu.SMEM)
VMEM = pl.BlockSpec(memory_space=pltpu.VMEM)
HBM = pl.BlockSpec(memory_space=pltpu.HBM)


def matmul(left, right):
    return jnp.dot(left, right, preferred_element_type=f32)


def operators_kernel(tallies, sink, source, own, *refs):
    counts, (f_ref, e_ref, own_ref, told_ref) = refs[:tallies], refs[tallies:]
    own_ref[...] = own[...]
    for number, count in enumerate(counts):
        told_ref[number] = jnp.full(told_ref.shape[1:], count[0], jnp.int32).astype(f32)
    n = sink.shape[-1]
    row = lax.broadcasted_iota(jnp.int32, (2 * n, 2 * n), 0)
    col = lax.broadcasted_iota(jnp.int32, (2 * n, 2 * n), 1)
    spread = jnp.where(col == (row % 2) * n + row // 2, 1.0, 0.0).astype(bf16)
    gathered = jnp.where(row == (col % 2) * n + col // 2, 1.0, 0.0).astype(bf16)
    f_real, f_imag = source[0], source[1]
    stacked = (
        jnp.concatenate([jnp.concatenate([f_real, f_imag], 1), jnp.concatenate([-f_imag, f_real], 1)], 0),
        jnp.concatenate([jnp.concatenate([f_imag, -f_real], 1), jnp.concatenate([f_real, f_imag], 1)], 0),
    )
    for part in range(2):
        rows = matmul(spread, stacked[part]).astype(bf16)
        f_ref[2 * n * part : 2 * n * (part + 1), :] = matmul(rows, gathered).astype(bf16)
    e_real, e_imag = sink[0], sink[1]
    e_ref[:n, :n] = e_real
    e_ref[:n, n:] = -e_imag
    e_ref[n:, :n] = e_imag
    e_ref[n:, n:] = e_real


def operators(sink, source, own, counts):
    n = source.shape[-1]
    return pl.pallas_call(
        functools.partial(operators_kernel, len(counts)),
        out_shape=(
            jax.ShapeDtypeStruct((4 * n, 2 * n), bf16),
            jax.ShapeDtypeStruct((2 * n, 2 * n), bf16),
            jax.ShapeDtypeStruct(own.shape, bf16),
            jax.ShapeDtypeStruct((max(len(counts), 1), 8, 128), f32),
        ),
        in_specs=[VMEM] * 3 + [SMEM] * len(counts),
        out_specs=[VMEM] * 4,
        cost_estimate=pl.CostEstimate(flops=10**8, bytes_accessed=10**6, transcendentals=0),
        compiler_params=pltpu.CompilerParams(vmem_limit_bytes=8 * 2**20),
        name="operators",
    )(sink, source, own, *counts)


def cut_kernel(steps, count_hbm, operator_hbm, columns_ref, sink_ref, source_ref, *refs):
    blocks, refs = refs[: len(steps)], refs[len(steps) :]
    sink, source, count_ref, operator_ref, count_sem, operator_sem, pair_sems, sems = refs
    rank = lax.axis_index("ta")
    sinks = sink_ref.shape[1]
    source_index, sink_index = rank // sinks, rank % sinks
    operator = pltpu.make_async_copy(operator_hbm, operator_ref, operator_sem)
    operator.start()
    copies = [pltpu.make_async_copy(count_hbm, count_ref, count_sem)]
    for number, (step, block) in enumerate(zip(steps, blocks)):
        copies.append(pltpu.make_async_copy(columns_ref.at[rank ^ step_mask(step, rank)], block.at[0], sems.at[number]))
    copies.append(pltpu.make_async_copy(source_ref.at[source_index], source, pair_sems.at[0]))
    for copy in copies:
        copy.start()
    operator.wait()
    chosen = operator_ref[0, sink_index] * NDISP + operator_ref[1, sink_index]
    copies.append(pltpu.make_async_copy(sink_ref.at[chosen, sink_index], sink, pair_sems.at[1]))
    copies[-1].start()
    for copy in copies:
        copy.wait()
    if not blocks:
        return
    count = count_ref[0]
    _, capacity, parts, order = blocks[0].shape

    @pl.when(count < capacity)
    def _():
        row = lax.broadcasted_iota(jnp.int32, (parts, order), 0)
        mark = jnp.where(row == 0, jnp.inf, count.astype(f32)).astype(bf16)
        for block in blocks:
            block[0, capacity - 1] = mark


def cut_blocks(counts, sink_operator, columns, sink_elemental, source_elemental, steps):
    _, capacity, parts, order = columns.shape
    pair_shape = jax.ShapeDtypeStruct(source_elemental.shape[1:], bf16)
    *blocks, sink, source = pl.pallas_call(
        functools.partial(cut_kernel, steps),
        out_shape=[jax.ShapeDtypeStruct((1, capacity, parts, order), bf16)] * len(steps) + [pair_shape] * 2,
        in_specs=[HBM] * 5,
        out_specs=[VMEM] * (len(steps) + 2),
        scratch_shapes=[
            pltpu.SMEM(counts.shape, jnp.int32),
            pltpu.SMEM(sink_operator.shape, jnp.int32),
            pltpu.SemaphoreType.DMA,
            pltpu.SemaphoreType.DMA,
            pltpu.SemaphoreType.DMA((2,)),
            pltpu.SemaphoreType.DMA((max(len(steps), 1),)),
        ],
        cost_estimate=pl.CostEstimate(flops=0, bytes_accessed=3 * 10**6, transcendentals=0),
        compiler_params=pltpu.CompilerParams(vmem_limit_bytes=60 * 2**20),
        name="cut_blocks",
    )(counts, sink_operator, columns, sink_elemental, source_elemental)
    return blocks, sink, source


def place_blocks(table, sources, arrays, packed):
    spins, _, _, n = packed.shape
    unroll = 8

    def place(array, index, batch):
        count, start = table[0, batch], table[1, batch]

        def one(column, carry):
            value = array[index, column]
            for spin in range(spins):
                packed[spin, start + column] = value[:, n * spin : n * (spin + 1)]
            return carry

        def several(group, carry):
            for column in range(unroll):
                one(group * unroll + column, carry)
            return carry

        whole = count // unroll
        lax.fori_loop(0, whole, several, 0)
        lax.fori_loop(whole * unroll, count, one, 0)

    for array, batch in zip(arrays, sources):
        if batch is None:
            lax.fori_loop(0, array.shape[0], lambda batch, carry, array=array: (place(array, batch, batch), carry)[1], 0)
        else:
            place(array, 0, batch)


def pair_kernel(batches_of, *refs):
    f_ref, e_ref, told_ref, *arrays = refs[:-7]
    out_hbm, packed, turned, right, result, table, sems = refs[-7:]
    spins, order, _, n = packed.shape
    if batches_of is None:
        *arrays, counts = arrays
        sources = [None]
        pltpu.sync_copy(counts, table.at[0])
    else:
        sources = batches_of(lax.axis_index("ta"))
        for number, (batch, array) in enumerate(zip(sources, arrays)):
            _, capacity, _, _ = array.shape
            if 1 <= number <= LEAD:
                told = told_ref[number - 1]
            else:
                last = array[0, capacity - 1, :, :128].astype(f32)
                told = jnp.where(last[:1] == jnp.inf, last[1:], float(capacity))
            table[0, batch] = told[0, 0].astype(jnp.int32)

    def running(batch, start):
        table[1, batch] = start
        return start + table[0, batch]

    lax.fori_loop(0, table.shape[1], running, jnp.int32(0))
    place_blocks(table, sources, arrays, packed)
    rows = packed.reshape(spins, 2 * order, n)
    half, per_half = order // 2, spins // 2
    for spin in range(spins):
        turned[n * spin : n * (spin + 1), :] = rows[spin].T
    copies = []
    for side in range(2):
        mine = slice(half * side, half * (side + 1))
        for spin in range(spins):
            near = slice(2 * n * spin, 2 * n * (spin + 1))
            column = jnp.concatenate([rows[per_half * side + k, near, :] for k in range(per_half)], axis=1)
            product = matmul(f_ref[...], column).astype(bf16)
            right[side, near, :half] = product[: 2 * n]
            right[side, near, half:] = product[2 * n :]
        total = matmul(turned[...], right[side]).astype(bf16)
        for spin in range(spins):
            here = slice(n * spin, n * (spin + 1))
            middle = jnp.concatenate([total[here, :half], total[here, half:]], axis=0)
            outcome = matmul(e_ref[...], middle)
            if (spin < per_half) != (side == 0):
                outcome = -outcome
            for part in range(2):
                result[part, here, mine] = outcome[n * part : n * (part + 1)].astype(bf16)
        copies.append(pltpu.make_async_copy(result.at[:, :, mine], out_hbm.at[:, :, mine], sems.at[side]))
        copies[-1].start()
    for copy in copies:
        copy.wait()


def pair_loop(batches_of, arrays, f_matrix, e_matrix, told, batches, order):
    n = order // SPINS
    return pl.pallas_call(
        functools.partial(pair_kernel, batches_of),
        out_shape=jax.ShapeDtypeStruct((2, order, order), bf16),
        in_specs=[VMEM] * (len(arrays) + 3),
        out_specs=HBM,
        scratch_shapes=[
            pltpu.VMEM((SPINS, order, 2, n), bf16),
            pltpu.VMEM((order, 2 * order), bf16),
            pltpu.VMEM((2, 2 * order, order), bf16),
            pltpu.VMEM((2, order, order), bf16),
            pltpu.SMEM((2, batches), jnp.int32),
            pltpu.SemaphoreType.DMA((2,)),
        ],
        cost_estimate=pl.CostEstimate(flops=2 * 10**9, bytes_accessed=3 * 10**6, transcendentals=0),
        compiler_params=pltpu.CompilerParams(vmem_limit_bytes=24 * 2**20),
        name="pair_loop",
    )(f_matrix, e_matrix, told, *arrays)


OWN = (0, 0, 1)


def exchange_steps(devices):
    far, near, low = list(range(devices // 2, devices)), [], devices // 4
    while low > 1:
        near += range(low, 2 * low)
        low //= 2
    steps = [(far[0], far[0], 1)]
    for number, (a, b) in enumerate(zip(far[1:-1], near)):
        classes = [c for c in range(1, devices) if parity(c & a) == 0 and parity(c & b) == 0]
        c = max(classes, key=lambda c: (c & 1, -bin(c).count("1"), c))
        steps += [(a, b, c), (b, a, c)]
        if number == devices // 4 - 1:
            steps.append((1, 1, 1))
    return steps + [(far[-1], far[-1], 1)]


def parity(value):
    return bin(value).count("1") % 2


def step_mask(step, rank):
    even, odd, class_mask = step
    if even == odd:
        return even
    folded, bit = 0, 0
    while class_mask >> bit:
        if class_mask >> bit & 1:
            folded = folded ^ (rank >> bit)
        bit += 1
    return jnp.where(folded & 1 == 0, even, odd)


def step_pairs(step, devices):
    even, odd, class_mask = step
    return [(i, i ^ (odd if parity(i & class_mask) else even)) for i in range(devices)]


def exchange(outgoing, counts, rank, cut):
    devices = outgoing.shape[0]
    steps = exchange_steps(devices)
    blocks = [lax.dynamic_slice_in_dim(outgoing, rank ^ step_mask(step, rank), 1) for step in steps[:LEAD]]
    (own, *others), sink, source = cut([OWN] + steps[LEAD:])
    tallies = []
    for step in steps[:LEAD]:
        tallies.append(lax.ppermute(counts, "ta", step_pairs(step, devices)))
    received = []
    for step, block in zip(steps, blocks + others):
        received.append(lax.ppermute(block, "ta", step_pairs(step, devices)))
    f_matrix, e_matrix, own, told = operators(sink, source, own, tallies)
    return [own] + received, f_matrix, e_matrix, told, lambda me: [me ^ step_mask(step, me) for step in [OWN] + steps]


def local(perambulator, batch_columns, sink_operator, sink_elemental, source_elemental):
    source_count, sink_count, capacity, parts, order = perambulator.shape
    devices = lax.axis_size("ta")
    assert source_count * sink_count == devices
    rank = lax.axis_index("ta").astype(jnp.int32)
    outgoing = perambulator.reshape(devices, capacity, parts, order)
    cut = functools.partial(cut_blocks, batch_columns, sink_operator, outgoing, sink_elemental, source_elemental)
    if exchanged(devices):
        arrays, f_matrix, e_matrix, told, batches_of = exchange(outgoing, batch_columns, rank, cut)
    else:
        _, sink, source = cut([])
        arrays = [lax.all_to_all(outgoing, "ta", split_axis=0, concat_axis=0, tiled=True)]
        arrays.append(lax.all_gather(batch_columns, "ta", axis=0, tiled=True))
        f_matrix, e_matrix, _, told = operators(sink, source, sink, [])
        batches_of = None
    return pair_loop(batches_of, arrays, f_matrix, e_matrix, told, devices, order)[None]


def exchanged(devices):
    return 8 <= devices <= LARGEST_EXCHANGE and devices & (devices - 1) == 0


def solution(mesh):
    placed = (
        P("grp", None, "ta", None, None),
        P(("grp", "ta")),
        P(),
        P("grp", None, None, None, None),
        P("grp", None, None, None),
    )
    return jax.shard_map(
        local,
        mesh=mesh,
        in_specs=placed,
        out_specs=P(("grp", "ta"), None, None, None),
        check_vma=False,
    )
```

```python
import functools

import jax
import jax.numpy as jnp
from jax import lax
from jax.experimental import pallas as pl
from jax.experimental.pallas import tpu as pltpu
from jax.sharding import PartitionSpec as P

NDISP = 2
SPINS = 4
LARGEST_EXCHANGE = 32
LEAD = 2

f32 = jnp.float32
bf16 = jnp.bfloat16

SMEM = pl.BlockSpec(memory_space=pltpu.SMEM)
VMEM = pl.BlockSpec(memory_space=pltpu.VMEM)
HBM = pl.BlockSpec(memory_space=pltpu.HBM)


def matmul(left, right):
    return jnp.dot(left, right, preferred_element_type=f32)


def operators_kernel(tallies, sink, source, own, *refs):
    counts, (f_ref, e_ref, own_ref, told_ref) = refs[:tallies], refs[tallies:]
    own_ref[...] = own[...]
    for number, count in enumerate(counts):
        told_ref[number] = jnp.full(told_ref.shape[1:], count[0], jnp.int32).astype(f32)
    n = sink.shape[-1]
    row = lax.broadcasted_iota(jnp.int32, (2 * n, 2 * n), 0)
    col = lax.broadcasted_iota(jnp.int32, (2 * n, 2 * n), 1)
    spread = jnp.where(col == (row % 2) * n + row // 2, 1.0, 0.0).astype(bf16)
    gathered = jnp.where(row == (col % 2) * n + col // 2, 1.0, 0.0).astype(bf16)
    f_real, f_imag = source[0], source[1]
    stacked = (
        jnp.concatenate([jnp.concatenate([f_real, f_imag], 1), jnp.concatenate([-f_imag, f_real], 1)], 0),
        jnp.concatenate([jnp.concatenate([f_imag, -f_real], 1), jnp.concatenate([f_real, f_imag], 1)], 0),
    )
    for part in range(2):
        rows = matmul(spread, stacked[part]).astype(bf16)
        f_ref[2 * n * part : 2 * n * (part + 1), :] = matmul(rows, gathered).astype(bf16)
    e_real, e_imag = sink[0], sink[1]
    e_ref[:n, :n] = e_real
    e_ref[:n, n:] = -e_imag
    e_ref[n:, :n] = e_imag
    e_ref[n:, n:] = e_real


def operators(sink, source, own, counts):
    n = source.shape[-1]
    return pl.pallas_call(
        functools.partial(operators_kernel, len(counts)),
        out_shape=(
            jax.ShapeDtypeStruct((4 * n, 2 * n), bf16),
            jax.ShapeDtypeStruct((2 * n, 2 * n), bf16),
            jax.ShapeDtypeStruct(own.shape, bf16),
            jax.ShapeDtypeStruct((max(len(counts), 1), 8, 128), f32),
        ),
        in_specs=[VMEM] * 3 + [SMEM] * len(counts),
        out_specs=[VMEM] * 4,
        cost_estimate=pl.CostEstimate(flops=10**8, bytes_accessed=10**6, transcendentals=0),
        compiler_params=pltpu.CompilerParams(vmem_limit_bytes=8 * 2**20),
        name="operators",
    )(sink, source, own, *counts)


def cut_kernel(steps, count_hbm, operator_hbm, columns_ref, sink_ref, source_ref, *refs):
    blocks, refs = refs[: len(steps)], refs[len(steps) :]
    sink, source, count_ref, operator_ref, count_sem, operator_sem, pair_sems, sems = refs
    rank = lax.axis_index("ta")
    sinks = sink_ref.shape[1]
    source_index, sink_index = rank // sinks, rank % sinks
    operator = pltpu.make_async_copy(operator_hbm, operator_ref, operator_sem)
    operator.start()
    copies = [pltpu.make_async_copy(count_hbm, count_ref, count_sem)]
    for number, (step, block) in enumerate(zip(steps, blocks)):
        copies.append(pltpu.make_async_copy(columns_ref.at[rank ^ step_mask(step, rank)], block.at[0], sems.at[number]))
    copies.append(pltpu.make_async_copy(source_ref.at[source_index], source, pair_sems.at[0]))
    for copy in copies:
        copy.start()
    operator.wait()
    chosen = operator_ref[0, sink_index] * NDISP + operator_ref[1, sink_index]
    copies.append(pltpu.make_async_copy(sink_ref.at[chosen, sink_index], sink, pair_sems.at[1]))
    copies[-1].start()
    for copy in copies:
        copy.wait()
    if not blocks:
        return
    count = count_ref[0]
    _, capacity, parts, order = blocks[0].shape

    @pl.when(count < capacity)
    def _():
        row = lax.broadcasted_iota(jnp.int32, (parts, order), 0)
        mark = jnp.where(row == 0, jnp.inf, count.astype(f32)).astype(bf16)
        for block in blocks:
            block[0, capacity - 1] = mark


def cut_blocks(counts, sink_operator, columns, sink_elemental, source_elemental, steps):
    _, capacity, parts, order = columns.shape
    pair_shape = jax.ShapeDtypeStruct(source_elemental.shape[1:], bf16)
    *blocks, sink, source = pl.pallas_call(
        functools.partial(cut_kernel, steps),
        out_shape=[jax.ShapeDtypeStruct((1, capacity, parts, order), bf16)] * len(steps) + [pair_shape] * 2,
        in_specs=[HBM] * 5,
        out_specs=[VMEM] * (len(steps) + 2),
        scratch_shapes=[
            pltpu.SMEM(counts.shape, jnp.int32),
            pltpu.SMEM(sink_operator.shape, jnp.int32),
            pltpu.SemaphoreType.DMA,
            pltpu.SemaphoreType.DMA,
            pltpu.SemaphoreType.DMA((2,)),
            pltpu.SemaphoreType.DMA((max(len(steps), 1),)),
        ],
        cost_estimate=pl.CostEstimate(flops=0, bytes_accessed=3 * 10**6, transcendentals=0),
        compiler_params=pltpu.CompilerParams(vmem_limit_bytes=8 * 2**20),
        name="cut_blocks",
    )(counts, sink_operator, *[pltpu.with_memory_space_constraint(x, pltpu.HBM) for x in (columns, sink_elemental, source_elemental)])
    return blocks, sink, source


def place_blocks(table, sources, arrays, packed):
    spins, _, _, n = packed.shape
    unroll = 8

    def place(array, index, batch):
        count, start = table[0, batch], table[1, batch]

        def move(first, columns):
            value = array[index, pl.ds(first, columns)]
            for spin in range(spins):
                packed[spin, pl.ds(start + first, columns)] = value[:, :, n * spin : n * (spin + 1)]

        def several(group, carry):
            move(jnp.minimum(group * unroll, count - unroll), unroll)
            return carry

        def one(column, carry):
            move(column, 1)
            return carry

        small = count < unroll
        if array.shape[1] >= unroll:
            lax.fori_loop(0, jnp.where(small, 0, (count + unroll - 1) // unroll), several, 0)
        lax.fori_loop(0, jnp.where(small, count, 0), one, 0)

    for array, batch in zip(arrays, sources):
        if batch is None:
            lax.fori_loop(0, array.shape[0], lambda batch, carry, array=array: (place(array, batch, batch), carry)[1], 0)
        else:
            place(array, 0, batch)


def pair_kernel(batches_of, *refs):
    f_ref, e_ref, told_ref, *arrays = refs[:-7]
    out_hbm, packed, turned, right, result, table, sems = refs[-7:]
    spins, order, _, n = packed.shape
    if batches_of is None:
        *arrays, counts = arrays
        sources = [None]
        pltpu.sync_copy(counts, table.at[0])
    else:
        sources = batches_of(lax.axis_index("ta"))
        for number, (batch, array) in enumerate(zip(sources, arrays)):
            _, capacity, _, _ = array.shape
            if 1 <= number <= LEAD:
                told = told_ref[number - 1]
            else:
                last = array[0, capacity - 1, :, :128].astype(f32)
                told = jnp.where(last[:1] == jnp.inf, last[1:], float(capacity))
            table[0, batch] = told[0, 0].astype(jnp.int32)

    def running(batch, start):
        table[1, batch] = start
        return start + table[0, batch]

    lax.fori_loop(0, table.shape[1], running, jnp.int32(0))
    place_blocks(table, sources, arrays, packed)
    rows = packed.reshape(spins, 2 * order, n)
    half, per_half = order // 2, spins // 2
    for spin in range(spins):
        turned[n * spin : n * (spin + 1), :] = rows[spin].T
    copies = []
    for side in range(2):
        mine = slice(half * side, half * (side + 1))
        for spin in range(spins):
            near = slice(2 * n * spin, 2 * n * (spin + 1))
            column = jnp.concatenate([rows[per_half * side + k, near, :] for k in range(per_half)], axis=1)
            product = matmul(f_ref[...], column).astype(bf16)
            right[side, near, :half] = product[: 2 * n]
            right[side, near, half:] = product[2 * n :]
        total = matmul(turned[...], right[side]).astype(bf16)
        for spin in range(spins):
            here = slice(n * spin, n * (spin + 1))
            middle = jnp.concatenate([total[here, :half], total[here, half:]], axis=0)
            outcome = matmul(e_ref[...], middle)
            if (spin < per_half) != (side == 0):
                outcome = -outcome
            for part in range(2):
                result[part, here, mine] = outcome[n * part : n * (part + 1)].astype(bf16)
        copies.append(pltpu.make_async_copy(result.at[:, :, mine], out_hbm.at[:, :, mine], sems.at[side]))
        copies[-1].start()
    for copy in copies:
        copy.wait()


def pair_loop(batches_of, arrays, f_matrix, e_matrix, told, batches, order):
    n = order // SPINS
    return pl.pallas_call(
        functools.partial(pair_kernel, batches_of),
        out_shape=jax.ShapeDtypeStruct((2, order, order), bf16),
        in_specs=[VMEM] * (len(arrays) + 3),
        out_specs=HBM,
        scratch_shapes=[
            pltpu.VMEM((SPINS, order, 2, n), bf16),
            pltpu.VMEM((order, 2 * order), bf16),
            pltpu.VMEM((2, 2 * order, order), bf16),
            pltpu.VMEM((2, order, order), bf16),
            pltpu.SMEM((2, batches), jnp.int32),
            pltpu.SemaphoreType.DMA((2,)),
        ],
        cost_estimate=pl.CostEstimate(flops=2 * 10**9, bytes_accessed=3 * 10**6, transcendentals=0),
        compiler_params=pltpu.CompilerParams(vmem_limit_bytes=24 * 2**20),
        name="pair_loop",
    )(f_matrix, e_matrix, told, *arrays)


OWN = (0, 0, 1)


def exchange_steps(devices):
    far, near = range(devices // 2, devices), range(2, devices // 2)
    steps = [(far[0], far[0], 1)]
    for number, (a, b) in enumerate(zip(far[1:-1], near)):
        classes = [c for c in range(1, devices) if parity(c & a) == 0 and parity(c & b) == 0]
        c = max(classes, key=lambda c: (c & 1, -bin(c).count("1"), c))
        steps += [(a, b, c), (b, a, c)]
        if number == devices // 4 - 1:
            steps.append((1, 1, 1))
    return steps + [(far[-1], far[-1], 1)]


def parity(value):
    return bin(value).count("1") % 2


def step_mask(step, rank):
    even, odd, class_mask = step
    if even == odd:
        return even
    folded, bit = 0, 0
    while class_mask >> bit:
        if class_mask >> bit & 1:
            folded = folded ^ (rank >> bit)
        bit += 1
    return jnp.where(folded & 1 == 0, even, odd)


def step_pairs(step, devices):
    even, odd, class_mask = step
    return [(i, i ^ (odd if parity(i & class_mask) else even)) for i in range(devices)]


def exchange(outgoing, counts, rank, cut):
    devices = outgoing.shape[0]
    steps = exchange_steps(devices)
    blocks = [lax.dynamic_slice_in_dim(outgoing, rank ^ step_mask(step, rank), 1) for step in steps[:LEAD]]
    (own, *others), sink, source = cut([OWN] + steps[LEAD:])
    tallies = []
    for step in steps[:LEAD]:
        tallies.append(lax.ppermute(counts, "ta", step_pairs(step, devices)))
    received = []
    for step, block in zip(steps, blocks + others):
        received.append(lax.ppermute(block, "ta", step_pairs(step, devices)))
    f_matrix, e_matrix, own, told = operators(sink, source, own, tallies)
    return [own] + received, f_matrix, e_matrix, told, lambda me: [me ^ step_mask(step, me) for step in [OWN] + steps]


def local(perambulator, batch_columns, sink_operator, sink_elemental, source_elemental):
    source_count, sink_count, capacity, parts, order = perambulator.shape
    devices = lax.axis_size("ta")
    assert source_count * sink_count == devices
    rank = lax.axis_index("ta").astype(jnp.int32)
    outgoing = perambulator.reshape(devices, capacity, parts, order)
    cut = functools.partial(cut_blocks, batch_columns, sink_operator, outgoing, sink_elemental, source_elemental)
    if exchanged(devices):
        arrays, f_matrix, e_matrix, told, batches_of = exchange(outgoing, batch_columns, rank, cut)
    else:
        _, sink, source = cut([])
        arrays = [lax.all_to_all(outgoing, "ta", split_axis=0, concat_axis=0, tiled=True)]
        arrays.append(lax.all_gather(batch_columns, "ta", axis=0, tiled=True))
        f_matrix, e_matrix, _, told = operators(sink, source, sink, [])
        batches_of = None
    return pair_loop(batches_of, arrays, f_matrix, e_matrix, told, devices, order)[None]


def exchanged(devices):
    return 8 <= devices <= LARGEST_EXCHANGE and devices & (devices - 1) == 0


def solution(mesh):
    placed = (
        P("grp", None, "ta", None, None),
        P(("grp", "ta")),
        P(),
        P("grp", None, None, None, None),
        P("grp", None, None, None),
    )
    return jax.shard_map(
        local,
        mesh=mesh,
        in_specs=placed,
        out_specs=P(("grp", "ta"), None, None, None),
        check_vma=False,
    )
```

```python
import functools

import jax
import jax.numpy as jnp
from jax import lax
from jax.experimental import pallas as pl
from jax.experimental.pallas import tpu as pltpu
from jax.sharding import PartitionSpec as P

NDISP = 2
SPINS = 4
LARGEST_EXCHANGE = 32
LEAD = 2
LATE = 1

f32 = jnp.float32
bf16 = jnp.bfloat16

SMEM = pl.BlockSpec(memory_space=pltpu.SMEM)
VMEM = pl.BlockSpec(memory_space=pltpu.VMEM)
HBM = pl.BlockSpec(memory_space=pltpu.HBM)


def matmul(left, right):
    return jnp.dot(left, right, preferred_element_type=f32)


def operators_kernel(tallies, sink, source, own, *refs):
    counts, (f_ref, e_ref, own_ref, told_ref) = refs[:tallies], refs[tallies:]
    own_ref[...] = own[...]
    for number, count in enumerate(counts):
        told_ref[number] = jnp.full(told_ref.shape[1:], count[0], jnp.int32).astype(f32)
    n = sink.shape[-1]
    row = lax.broadcasted_iota(jnp.int32, (2 * n, 2 * n), 0)
    col = lax.broadcasted_iota(jnp.int32, (2 * n, 2 * n), 1)
    spread = jnp.where(col == (row % 2) * n + row // 2, 1.0, 0.0).astype(bf16)
    gathered = jnp.where(row == (col % 2) * n + col // 2, 1.0, 0.0).astype(bf16)
    f_real, f_imag = source[0], source[1]
    stacked = (
        jnp.concatenate([jnp.concatenate([f_real, f_imag], 1), jnp.concatenate([-f_imag, f_real], 1)], 0),
        jnp.concatenate([jnp.concatenate([f_imag, -f_real], 1), jnp.concatenate([f_real, f_imag], 1)], 0),
    )
    for part in range(2):
        rows = matmul(spread, stacked[part]).astype(bf16)
        f_ref[2 * n * part : 2 * n * (part + 1), :] = matmul(rows, gathered).astype(bf16)
    e_real, e_imag = sink[0], sink[1]
    e_ref[:n, :n] = e_real
    e_ref[:n, n:] = -e_imag
    e_ref[n:, :n] = e_imag
    e_ref[n:, n:] = e_real


def operators(sink, source, own, counts):
    n = source.shape[-1]
    return pl.pallas_call(
        functools.partial(operators_kernel, len(counts)),
        out_shape=(
            jax.ShapeDtypeStruct((4 * n, 2 * n), bf16),
            jax.ShapeDtypeStruct((2 * n, 2 * n), bf16),
            jax.ShapeDtypeStruct(own.shape, bf16),
            jax.ShapeDtypeStruct((max(len(counts), 1), 8, 128), f32),
        ),
        in_specs=[VMEM] * 3 + [SMEM] * len(counts),
        out_specs=[VMEM] * 4,
        cost_estimate=pl.CostEstimate(flops=10**8, bytes_accessed=10**6, transcendentals=0),
        compiler_params=pltpu.CompilerParams(vmem_limit_bytes=8 * 2**20),
        name="operators",
    )(sink, source, own, *counts)


def cut_kernel(steps, count_hbm, operator_hbm, columns_ref, sink_ref, source_ref, *refs):
    blocks, refs = refs[: len(steps)], refs[len(steps) :]
    sink, source, count_ref, operator_ref, count_sem, operator_sem, pair_sems, sems = refs
    rank = lax.axis_index("ta")
    sinks = sink_ref.shape[1]
    source_index, sink_index = rank // sinks, rank % sinks
    operator = pltpu.make_async_copy(operator_hbm, operator_ref, operator_sem)
    operator.start()
    copies = [pltpu.make_async_copy(count_hbm, count_ref, count_sem)]
    for number, (step, block) in enumerate(zip(steps, blocks)):
        copies.append(pltpu.make_async_copy(columns_ref.at[rank ^ step_mask(step, rank)], block.at[0], sems.at[number]))
    copies.append(pltpu.make_async_copy(source_ref.at[source_index], source, pair_sems.at[0]))
    for copy in copies:
        copy.start()
    operator.wait()
    chosen = operator_ref[0, sink_index] * NDISP + operator_ref[1, sink_index]
    copies.append(pltpu.make_async_copy(sink_ref.at[chosen, sink_index], sink, pair_sems.at[1]))
    copies[-1].start()
    for copy in copies:
        copy.wait()
    if not blocks:
        return
    count = count_ref[0]
    _, capacity, parts, order = blocks[0].shape

    @pl.when(count < capacity)
    def _():
        row = lax.broadcasted_iota(jnp.int32, (parts, order), 0)
        mark = jnp.where(row == 0, jnp.inf, count.astype(f32)).astype(bf16)
        for block in blocks:
            block[0, capacity - 1] = mark


def cut_blocks(counts, sink_operator, columns, sink_elemental, source_elemental, steps):
    _, capacity, parts, order = columns.shape
    pair_shape = jax.ShapeDtypeStruct(source_elemental.shape[1:], bf16)
    *blocks, sink, source = pl.pallas_call(
        functools.partial(cut_kernel, steps),
        out_shape=[jax.ShapeDtypeStruct((1, capacity, parts, order), bf16)] * len(steps) + [pair_shape] * 2,
        in_specs=[HBM] * 5,
        out_specs=[VMEM] * (len(steps) + 2),
        scratch_shapes=[
            pltpu.SMEM(counts.shape, jnp.int32),
            pltpu.SMEM(sink_operator.shape, jnp.int32),
            pltpu.SemaphoreType.DMA,
            pltpu.SemaphoreType.DMA,
            pltpu.SemaphoreType.DMA((2,)),
            pltpu.SemaphoreType.DMA((max(len(steps), 1),)),
        ],
        cost_estimate=pl.CostEstimate(flops=0, bytes_accessed=3 * 10**6, transcendentals=0),
        compiler_params=pltpu.CompilerParams(vmem_limit_bytes=8 * 2**20),
        name="cut_blocks",
    )(counts, *[pltpu.with_memory_space_constraint(x, pltpu.HBM) for x in (sink_operator, columns, sink_elemental, source_elemental)])
    return blocks, sink, source


def place_blocks(spans, arrays, packed):
    spins, _, _, n = packed.shape
    unroll = 8

    def place(array, index, count, start):
        def move(first, columns):
            value = array[index, pl.ds(first, columns)]
            for spin in range(spins):
                packed[spin, pl.ds(start + first, columns)] = value[:, :, n * spin : n * (spin + 1)]

        def several(group, carry):
            move(jnp.minimum(group * unroll, count - unroll), unroll)
            return carry

        def one(column, carry):
            move(column, 1)
            return carry

        small = count < unroll
        if array.shape[1] >= unroll:
            lax.fori_loop(0, jnp.where(small, 0, (count + unroll - 1) // unroll), several, 0)
        lax.fori_loop(0, jnp.where(small, count, 0), one, 0)

    for array, span in zip(arrays, spans):
        if isinstance(span, tuple):
            place(array, 0, *span)
        else:

            def each(batch, carry, array=array, table=span):
                place(array, batch, table[0, batch], table[1, batch])
                return carry

            lax.fori_loop(0, array.shape[0], each, 0)


def early_kernel(batches_of, told_ref, *refs):
    *arrays, packed, late_ref, table = refs
    if batches_of is None:
        *arrays, counts = arrays
        sources = [None]
        pltpu.sync_copy(counts, table.at[0])
    else:
        sources, left = batches_of(lax.axis_index("ta")), packed.shape[1]
        for number, batch in enumerate(sources[:-LATE]):
            if 1 <= number <= LEAD:
                told = told_ref[number - 1]
            else:
                capacity = arrays[number].shape[1]
                last = arrays[number][0, capacity - 1, :, :128].astype(f32)
                told = jnp.where(last[:1] == jnp.inf, last[1:], float(capacity))
            count = told[0, 0].astype(jnp.int32)
            table[0, batch] = count
            left = left - count
        table[0, sources[-1]] = left

    def running(batch, start):
        table[1, batch] = start
        return start + table[0, batch]

    lax.fori_loop(0, table.shape[1], running, jnp.int32(0))
    for number, batch in enumerate(sources[len(arrays) :]):
        for row in range(2):
            late_ref[2 * number + row] = jnp.full(late_ref.shape[1:], table[row, batch], jnp.int32).astype(f32)
    place_blocks([(table[0, batch], table[1, batch]) if batch is not None else table for batch in sources], arrays, packed)


def pack_early(batches_of, arrays, told, batches, order):
    return pl.pallas_call(
        functools.partial(early_kernel, batches_of),
        out_shape=(
            jax.ShapeDtypeStruct((SPINS, order, 2, order // SPINS), bf16),
            jax.ShapeDtypeStruct((2 * LATE, 8, 128), f32),
        ),
        in_specs=[VMEM] * (len(arrays) + 1),
        out_specs=(VMEM, VMEM),
        scratch_shapes=[pltpu.SMEM((2, batches), jnp.int32)],
        cost_estimate=pl.CostEstimate(flops=10**8, bytes_accessed=10**6, transcendentals=0),
        compiler_params=pltpu.CompilerParams(vmem_limit_bytes=8 * 2**20),
        name="pack_early",
    )(told, *arrays)


def pair_kernel(f_ref, e_ref, late_ref, *refs):
    *arrays, _, packed, out_hbm, turned, right, result, sems = refs
    spins, order, _, n = packed.shape
    scalar = lambda row: late_ref[row][0, 0].astype(jnp.int32)
    place_blocks([(scalar(2 * number), scalar(2 * number + 1)) for number in range(len(arrays))], arrays, packed)
    rows = packed.reshape(spins, 2 * order, n)
    half, per_half = order // 2, spins // 2
    for spin in range(spins):
        turned[n * spin : n * (spin + 1), :] = rows[spin].T
    copies = []
    for side in range(2):
        mine = slice(half * side, half * (side + 1))
        for spin in range(spins):
            near = slice(2 * n * spin, 2 * n * (spin + 1))
            column = jnp.concatenate([rows[per_half * side + k, near, :] for k in range(per_half)], axis=1)
            product = matmul(f_ref[...], column).astype(bf16)
            right[side, near, :half] = product[: 2 * n]
            right[side, near, half:] = product[2 * n :]
        total = matmul(turned[...], right[side]).astype(bf16)
        for spin in range(spins):
            here = slice(n * spin, n * (spin + 1))
            middle = jnp.concatenate([total[here, :half], total[here, half:]], axis=0)
            outcome = matmul(e_ref[...], middle)
            if (spin < per_half) != (side == 0):
                outcome = -outcome
            for part in range(2):
                result[part, here, mine] = outcome[n * part : n * (part + 1)].astype(bf16)
        copies.append(pltpu.make_async_copy(result.at[:, :, mine], out_hbm.at[:, :, mine], sems.at[side]))
        copies[-1].start()
    for copy in copies:
        copy.wait()


def pair_loop(arrays, packed, f_matrix, e_matrix, late):
    _, order, _, _ = packed.shape
    return pl.pallas_call(
        pair_kernel,
        out_shape=(jax.ShapeDtypeStruct(packed.shape, bf16), jax.ShapeDtypeStruct((2, order, order), bf16)),
        in_specs=[VMEM] * (len(arrays) + 4),
        out_specs=(VMEM, HBM),
        scratch_shapes=[
            pltpu.VMEM((order, 2 * order), bf16),
            pltpu.VMEM((2, 2 * order, order), bf16),
            pltpu.VMEM((2, order, order), bf16),
            pltpu.SemaphoreType.DMA((2,)),
        ],
        input_output_aliases={3 + len(arrays): 0},
        cost_estimate=pl.CostEstimate(flops=2 * 10**9, bytes_accessed=3 * 10**6, transcendentals=0),
        compiler_params=pltpu.CompilerParams(vmem_limit_bytes=24 * 2**20),
        name="pair_loop",
    )(f_matrix, e_matrix, late, *arrays, packed)[1]


OWN = (0, 0, 1)


def exchange_steps(devices):
    far, near = range(devices // 2, devices), range(2, devices // 2)
    steps = [(far[0], far[0], 1)]
    for number, (a, b) in enumerate(zip(far[1:-1], near)):
        classes = [c for c in range(1, devices) if parity(c & a) == 0 and parity(c & b) == 0]
        c = max(classes, key=lambda c: (c & 1, -bin(c).count("1"), c))
        steps += [(a, b, c), (b, a, c)]
        if number == devices // 4 - 1:
            steps.append((1, 1, 1))
    return steps + [(far[-1], far[-1], 1)]


def parity(value):
    return bin(value).count("1") % 2


def step_mask(step, rank):
    even, odd, class_mask = step
    if even == odd:
        return even
    folded, bit = 0, 0
    while class_mask >> bit:
        if class_mask >> bit & 1:
            folded = folded ^ (rank >> bit)
        bit += 1
    return jnp.where(folded & 1 == 0, even, odd)


def step_pairs(step, devices):
    even, odd, class_mask = step
    return [(i, i ^ (odd if parity(i & class_mask) else even)) for i in range(devices)]


def exchange(outgoing, counts, rank, cut):
    devices = outgoing.shape[0]
    steps = exchange_steps(devices)
    blocks = [lax.dynamic_slice_in_dim(outgoing, rank ^ step_mask(step, rank), 1) for step in steps[:LEAD]]
    (own, *others), sink, source = cut([OWN] + steps[LEAD:])
    tallies = []
    for step in steps[:LEAD]:
        tallies.append(lax.ppermute(counts, "ta", step_pairs(step, devices)))
    received = []
    for step, block in zip(steps, blocks + others):
        received.append(lax.ppermute(block, "ta", step_pairs(step, devices)))
    f_matrix, e_matrix, own, told = operators(sink, source, own, tallies)
    return [own] + received, f_matrix, e_matrix, told, lambda me: [me ^ step_mask(step, me) for step in [OWN] + steps]


def local(perambulator, batch_columns, sink_operator, sink_elemental, source_elemental):
    source_count, sink_count, capacity, parts, order = perambulator.shape
    devices = lax.axis_size("ta")
    assert source_count * sink_count == devices
    rank = lax.axis_index("ta").astype(jnp.int32)
    outgoing = perambulator.reshape(devices, capacity, parts, order)
    cut = functools.partial(cut_blocks, batch_columns, sink_operator, outgoing, sink_elemental, source_elemental)
    late = []
    if exchanged(devices):
        arrays, f_matrix, e_matrix, told, batches_of = exchange(outgoing, batch_columns, rank, cut)
        arrays, late = arrays[:-LATE], arrays[-LATE:]
    else:
        _, sink, source = cut([])
        arrays = [lax.all_to_all(outgoing, "ta", split_axis=0, concat_axis=0, tiled=True)]
        arrays.append(lax.all_gather(batch_columns, "ta", axis=0, tiled=True))
        f_matrix, e_matrix, _, told = operators(sink, source, sink, [])
        batches_of = None
    packed, spans = pack_early(batches_of, arrays, told, devices, order)
    return pair_loop(late, packed, f_matrix, e_matrix, spans)[None]


def exchanged(devices):
    return 8 <= devices <= LARGEST_EXCHANGE and devices & (devices - 1) == 0


def solution(mesh):
    placed = (
        P("grp", None, "ta", None, None),
        P(("grp", "ta")),
        P(),
        P("grp", None, None, None, None),
        P("grp", None, None, None),
    )
    return jax.shard_map(
        local,
        mesh=mesh,
        in_specs=placed,
        out_specs=P(("grp", "ta"), None, None, None),
        check_vma=False,
    )
```
